768 devices in a mesh: tm: 24 (over z_hi, y), head: 32 (over z_lo, x, core).
Axes of the slice: x: 4, y: 8, z: 12 (z_hi: 3, z_lo: 4; z = z_hi * 4 + z_lo), core: 2. Of those that a mesh axis runs over, the one named last changes fastest.
Arguments:
- queries: bfloat16 [49152, 4096], P('tm', 'head'), may hold values from -64 to 64
- saved_keys: bfloat16 [49152, 4096], P('tm', 'head'), may hold values from -16 to 16
- saved_values: bfloat16 [49152, 4096], P('tm', 'head'), may hold values from -6 to 6
- out_grad: bfloat16 [49152, 4096], P(('tm', 'head')), may hold values from -6 to 6
- radius: int32 [32], P('head'), may hold values from 0 to 2, as said below
- clip_ids: int32 [192], replicated, may hold values from 0 to 31, never falling along the last dimension, each value on 1 to 12 neighbouring positions
Outputs:
- grad_queries: bfloat16 [49152, 4096], P('tm', 'head')
- grad_keys: bfloat16 [49152, 4096], P('tm', 'head')
- grad_values: bfloat16 [49152, 4096], P('tm', 'head')
The draws below stay inside these ranges and needn't reach their ends.
Inputs may be any that keep to these rules, and one draw needn't show every extreme that they name: Some head has radius exactly 2 and some head radius 0.
All inputs are finite; a program needn't handle non-finite values.
Results may differ from the reference program's by a relative error of at most 0.012.
Values may be sent and summed in bfloat16 or wider, within the bound.
No kernel may reach another device: no remote copies, remote signals or barrier semaphores. Data moves between devices by JAX's collectives and lax.ppermute only.
A program may use at most 64 MiB of HBM per device.

```python
import math
import jax
import jax.numpy as jnp
import numpy as np
from jax import lax

HEADS = 32
HD = 128
FRAME = 256
RADIUS = 2
D = 4096
FRAMES = 192
TOKENS = 49152


def draw_pair(key):
    base_key = jax.random.fold_in(key, 11)
    key_rows = jax.random.normal(jax.random.fold_in(base_key, 1), (TOKENS, HEADS, HD), jnp.float32)
    query_rows = jax.random.normal(jax.random.fold_in(base_key, 2), (TOKENS, HEADS, HD), jnp.float32)
    query_rows = jnp.clip(query_rows, -6.0, 6.0)
    key_rows = jnp.clip(key_rows, -6.0, 6.0)
    return (query_rows.reshape(TOKENS, HEADS * HD).astype(jnp.bfloat16), key_rows.reshape(TOKENS, HEADS * HD).astype(jnp.bfloat16))


def draw_queries(key, part):
    return draw_pair(key)[0]


def draw_saved_keys(key, part):
    return draw_pair(key)[1]


def draw_radius(key, part):
    values = jax.random.randint(key, (HEADS,), 0, RADIUS + 1, jnp.int32)
    chosen = jax.random.randint(jax.random.fold_in(key, 1), (), 0, HEADS, jnp.int32)
    other = (chosen + 1 + jax.random.randint(jax.random.fold_in(key, 2), (), 0, HEADS - 1, jnp.int32)) % HEADS
    values = values.at[chosen].set(RADIUS)
    values = values.at[other].set(0)
    return values.astype(jnp.int32)


def levels(stream_key, shape, pieces, low, high):
    level = 1.0
    for position, parts in pieces:
        steps = jax.random.uniform(jax.random.fold_in(jax.random.fold_in(stream_key, 6), position), (parts,), jnp.float32, low / len(pieces), high / len(pieces))
        level = level * jnp.repeat(jnp.exp(steps), shape[position] // parts).reshape((-1,) + (1,) * (len(shape) - 1 - position))
    return level


def profile(amount, total, reach, slope):
    portions = [(1 << 20) // math.isqrt(standing ** slope) + 1 for standing in range(2, amount + 1)]
    spare, given = total - reach - (amount - 1), [1] * (amount - 1)
    while spare > 0:
        candidates = [i for i in range(amount - 1) if given[i] < reach]
        whole, remaining = sum([portions[i] for i in candidates]), spare
        for i in candidates:
            more = min(reach - given[i], max(1, remaining * portions[i] // whole), spare)
            given[i] = given[i] + more
            spare = spare - more
    return np.array([reach] + given)


def uneven_parts(stream_key, number_of, total, reach, slope):
    if number_of == 2:
        one = jax.random.randint(stream_key, (), max(1, total - reach), min(reach, total - 1) + 1)
        return jnp.stack([one, total - one])
    sizes = jnp.asarray(profile(number_of, total, reach, slope), jnp.int32)
    pairs = (number_of - 1) // 2
    giver, sink = sizes[1:1 + 2 * pairs:2], sizes[2:2 + 2 * pairs:2]
    margin = jnp.minimum(giver - 1, reach - sink)
    shifted = jax.random.randint(jax.random.fold_in(stream_key, 1), (pairs,), 0, 1 << 20) % (margin + 1)
    sizes = sizes.at[1:1 + 2 * pairs:2].set(giver - shifted).at[2:2 + 2 * pairs:2].set(sink + shifted)
    return sizes[jax.random.permutation(jax.random.fold_in(stream_key, 2), number_of)]


def centred(own_key, dims, scale, most, cuts=(), kind=jnp.bfloat16):
    factor_of = levels(own_key, dims, cuts, -0.22, 0.18) if cuts else 1.0
    values = jax.random.normal(own_key, dims, jnp.float32) * scale * factor_of
    return jnp.minimum(jnp.maximum(values, -most), most).astype(kind)


def setup_inputs(seed: int = 0) -> dict:
    key_of = jax.random.split(jax.random.key(seed), 7)
    queries = draw_queries(jax.random.fold_in(key_of[6], 71), 0)
    saved_keys = draw_saved_keys(jax.random.fold_in(key_of[6], 71), 0)
    saved_values = centred(key_of[2], (TOKENS, D), 1.0, 6.0, ((0, 24), (1, 32)))
    out_grad = centred(key_of[3], (TOKENS, D), 1.0, 6.0, ((0, 768),))
    radius = draw_radius(jax.random.fold_in(key_of[6], 71), 0)
    clip_ids = jnp.searchsorted(jnp.cumsum(uneven_parts(key_of[5], FRAMES // 6, FRAMES, 12, 0)), jnp.arange(FRAMES), side="right").astype(jnp.int32)
    return dict(queries=queries, saved_keys=saved_keys, saved_values=saved_values, out_grad=out_grad, radius=radius, clip_ids=clip_ids)


def reference(queries, saved_keys, saved_values, out_grad, radius, clip_ids):
    span = 2 * RADIUS + 1
    scale = HD ** -0.5

    def one_head(head_index):
        start = (head_index * HD).astype(jnp.int32)

        def columns(whole):
            return lax.dynamic_slice_in_dim(whole, start, HD, 1).astype(jnp.float32).reshape(FRAMES, FRAME, HD)

        query_part = columns(queries)
        key_part = columns(saved_keys)
        value_part = columns(saved_values)
        grad_part = columns(out_grad)
        padding = ((RADIUS, RADIUS), (0, 0), (0, 0))
        key_padded = jnp.pad(key_part, padding)
        value_padded = jnp.pad(value_part, padding)
        key_window = jnp.stack([key_padded[offset:offset + FRAMES] for offset in range(span)], 1)
        value_window = jnp.stack([value_padded[offset:offset + FRAMES] for offset in range(span)], 1)
        frame_index = jnp.arange(FRAMES, dtype=jnp.int32)
        steps_away = jnp.arange(span, dtype=jnp.int32) - RADIUS
        key_frame = frame_index[:, None] + steps_away[None, :]
        inside = (key_frame >= 0) & (key_frame < FRAMES)
        key_clip = clip_ids[jnp.clip(key_frame, 0, FRAMES - 1)]
        within = jnp.abs(steps_away) <= radius[head_index]
        valid = inside & (clip_ids[:, None] == key_clip) & within[None, :]
        scores = jnp.einsum('aqd,ajkd->aqjk', query_part, key_window) * scale
        scores = jnp.where(valid[:, None, :, None], scores, -1e30)
        highest = jnp.max(scores, axis=(2, 3), keepdims=True)
        expo = jnp.exp(scores - highest)
        probs = expo / jnp.sum(expo, axis=(2, 3), keepdims=True)
        probs_b = probs.astype(jnp.bfloat16).astype(jnp.float32)
        dprobs = jnp.einsum('aqd,ajkd->aqjk', grad_part, value_window)
        delta = jnp.sum(probs * dprobs, axis=(2, 3), keepdims=True)
        dscores = (probs * (dprobs - delta)).astype(jnp.bfloat16).astype(jnp.float32)
        grad_query = jnp.einsum('aqjk,ajkd->aqd', dscores, key_window) * scale
        key_terms = jnp.einsum('aqjk,aqd->ajkd', dscores, query_part) * scale
        value_terms = jnp.einsum('aqjk,aqd->ajkd', probs_b, grad_part)
        key_total = sum(jnp.pad(key_terms[:, offset], ((offset, span - 1 - offset), (0, 0), (0, 0))) for offset in range(span))
        value_total = sum(jnp.pad(value_terms[:, offset], ((offset, span - 1 - offset), (0, 0), (0, 0))) for offset in range(span))
        grad_key = key_total[RADIUS:RADIUS + FRAMES]
        grad_value = value_total[RADIUS:RADIUS + FRAMES]
        return (grad_query.reshape(TOKENS, HD).astype(jnp.bfloat16),
                grad_key.reshape(TOKENS, HD).astype(jnp.bfloat16),
                grad_value.reshape(TOKENS, HD).astype(jnp.bfloat16))

    grad_q, grad_k, grad_v = lax.map(one_head, jnp.arange(HEADS, dtype=jnp.int32))

    def arrange(stacked):
        return jnp.transpose(stacked, (1, 0, 2)).reshape(TOKENS, HEADS * HD)

    return (arrange(grad_q), arrange(grad_k), arrange(grad_v))
```

```python
import functools

import jax
import jax.numpy as jnp
from jax import lax
from jax.experimental import pallas as pl
from jax.experimental.pallas import tpu as pltpu
from jax.sharding import PartitionSpec as P


FRAME = 256
RADIUS = 2
SPAN = 2 * RADIUS + 1
NEG = -1e30
LOG2E = 1.4426950408889634
STAT_ROWS = 48

NT = (((1,), (1,)), ((), ()))
NN = (((1,), (0,)), ((), ()))


def dot(a, b, dims):
    return lax.dot_general(a, b, dims, preferred_element_type=jnp.float32)


def frame_rows(index):
    return pl.ds(pl.multiple_of(index * FRAME, FRAME), FRAME)


def make_allowed(where_ref, radius_ref, clip_ref, count):
    first = where_ref[0] * count
    total = clip_ref.shape[0]
    radius = radius_ref[0]

    def allowed(query, key):
        fq = first + query
        fk = first + key
        inside = (fq >= 0) & (fq < total) & (fk >= 0) & (fk < total)
        cq = clip_ref[jnp.clip(fq, 0, total - 1)]
        ck = clip_ref[jnp.clip(fk, 0, total - 1)]
        return inside & (jnp.abs(fq - fk) <= radius) & (cq == ck)

    return allowed


def stats_kernel(count, where_ref, radius_ref, clip_ref, q_ref, k_ref, v_ref, g_ref, odd_ref, even_ref, e_scr, row_scr):
    width = q_ref.shape[1]
    c = width**-0.5 * LOG2E
    allowed = make_allowed(where_ref, radius_ref, clip_ref, count)
    parity = lax.rem(where_ref[0], 2)
    row_scr[...] = jnp.zeros_like(row_scr)
    for slot, out in ((0, odd_ref), (1, even_ref)):
        side = parity if slot == 0 else 1 - parity
        base_q = side * (count - RADIUS)
        base_k = side * (count - 2 * RADIUS)
        for i in range(RADIUS):
            qf = base_q + i
            q = q_ref[frame_rows(qf), :]
            g = g_ref[frame_rows(qf), :]
            out[i * FRAME : (i + 1) * FRAME, :] = g
            top = None
            for j in range(2 * RADIUS):
                s = dot(k_ref[frame_rows(base_k + j), :], q, NT)
                s = jnp.where(allowed(qf, base_k + j), s, NEG)
                e_scr[j] = s
                peak = jnp.max(s, axis=0, keepdims=True)
                top = peak if top is None else jnp.maximum(top, peak)
            total = jnp.zeros_like(top)
            delta = jnp.zeros_like(top)
            for j in range(2 * RADIUS):
                e = jnp.exp2((e_scr[j] - top) * c)
                dp = dot(v_ref[frame_rows(base_k + j), :], g, NT)
                total = total + jnp.sum(e, axis=0, keepdims=True)
                delta = delta + jnp.sum(e * dp, axis=0, keepdims=True)
            row = i * 18
            for stat in (top, total, delta):
                rest = stat
                for _ in range(3):
                    part = rest.astype(jnp.bfloat16).astype(jnp.float32)
                    rest = rest - part
                    row_scr[row : row + 1, :] = part[:, :128]
                    row_scr[row + 1 : row + 2, :] = part[:, 128:]
                    row += 2
        out[RADIUS * FRAME :, :] = row_scr[...].astype(jnp.bfloat16)


def main_kernel(
    count,
    where_ref,
    radius_ref,
    clip_ref,
    q_ref,
    k_ref,
    v_ref,
    g_ref,
    odd_ref,
    even_ref,
    relay_ref,
    godd_ref,
    geven_ref,
    dq_ref,
    dk_ref,
    dv_ref,
    kx,
    vx,
    qx,
    gx,
    kt,
    dk_acc,
    dv_acc,
    e_scr,
    dp_scr,
    stat_scr,
):
    width = q_ref.shape[1]
    scale = width**-0.5
    c = scale * LOG2E
    rim = RADIUS * FRAME
    own = count * FRAME
    allowed = make_allowed(where_ref, radius_ref, clip_ref, count)
    parity = lax.rem(where_ref[0], 2)
    kx[pl.ds(rim, own), :] = k_ref[...]
    vx[pl.ds(rim, own), :] = v_ref[...]
    far = where_ref[1]
    for slot, kvq, gs in ((0, odd_ref, godd_ref), (1, even_ref, geven_ref)):
        after = parity if slot == 0 else 1 - parity
        dst = pl.ds(pl.multiple_of(after * (rim + own), rim), rim)
        half = pl.ds(pl.multiple_of(after * rim, rim), rim)
        kx[dst, :] = kvq[0:rim, :]
        vx[dst, :] = kvq[rim : 2 * rim, :]
        qx[half, :] = kvq[2 * rim : 3 * rim, :]
        if slot == 0:

            @pl.when(far == 1)
            def _():
                vx[dst, :] = relay_ref[0:rim, :]
                qx[half, :] = relay_ref[rim : 2 * rim, :]

        gx[half, :] = gs[0:rim, :]
        stat_scr[pl.ds(pl.multiple_of(after * STAT_ROWS, 8), STAT_ROWS), :] = gs[rim:, :].astype(jnp.float32)
    for f in range(count + 2 * RADIUS):
        kt[:, f * FRAME : (f + 1) * FRAME] = kx[f * FRAME : (f + 1) * FRAME, :].T
    dk_acc[...] = jnp.zeros_like(dk_acc)
    dv_acc[...] = jnp.zeros_like(dv_acc)

    def one_query_frame(a, carry):
        q = q_ref[frame_rows(a), :]
        g = g_ref[frame_rows(a), :]
        top = None
        for j in range(SPAN):
            s = dot(kx[frame_rows(a + j), :], q, NT)
            s = jnp.where(allowed(a, a + j - RADIUS), s, NEG)
            e_scr[j] = s
            peak = jnp.max(s, axis=0, keepdims=True)
            top = peak if top is None else jnp.maximum(top, peak)
        total = jnp.zeros_like(top)
        delta = jnp.zeros_like(top)
        for j in range(SPAN):
            e = jnp.exp2((e_scr[j] - top) * c)
            dp = dot(vx[frame_rows(a + j), :], g, NT)
            total = total + jnp.sum(e, axis=0, keepdims=True)
            delta = delta + jnp.sum(e * dp, axis=0, keepdims=True)
            e_scr[j] = e
            dp_scr[j] = dp
        inverse = 1.0 / total
        delta = delta * inverse
        dqt = None
        for j in range(SPAN):
            p = e_scr[j] * inverse
            ds = (p * (dp_scr[j] - delta)).astype(jnp.bfloat16)
            rows = frame_rows(a + j)
            dv_acc[rows, :] += dot(p.astype(jnp.bfloat16), g, NN)
            dk_acc[rows, :] += dot(ds, q, NN)
            part = dot(kt[:, rows], ds, NN)
            dqt = part if dqt is None else dqt + part
        dq_ref[frame_rows(a), :] = (dqt * scale).T.astype(jnp.bfloat16)
        return carry

    lax.fori_loop(0, count, one_query_frame, 0)

    for h in range(2 * RADIUS):
        side, i = divmod(h, RADIUS)
        if side == 0:
            qf = i - RADIUS
            keys = list(range(0, i + 1))
        else:
            qf = count + i
            keys = list(range(count - RADIUS + i, count))
        q = qx[h * FRAME : (h + 1) * FRAME, :]
        g = gx[h * FRAME : (h + 1) * FRAME, :]
        stats = []
        row = side * STAT_ROWS + i * 18
        for _ in range(3):
            halves = []
            for lane in range(2):
                halves.append(
                    stat_scr[row + lane : row + lane + 1, :]
                    + stat_scr[row + 2 + lane : row + 3 + lane, :]
                    + stat_scr[row + 4 + lane : row + 5 + lane, :]
                )
            stats.append(jnp.concatenate(halves, axis=1))
            row += 6
        far_top, far_total, far_delta = stats
        top = far_top
        for n, f in enumerate(keys):
            s = dot(k_ref[f * FRAME : (f + 1) * FRAME, :], q, NT)
            s = jnp.where(allowed(qf, f), s, NEG)
            e_scr[n] = s
            top = jnp.maximum(top, jnp.max(s, axis=0, keepdims=True))
        fade = jnp.exp2((far_top - top) * c)
        total = far_total * fade
        delta = far_delta * fade
        for n, f in enumerate(keys):
            e = jnp.exp2((e_scr[n] - top) * c)
            dp = dot(v_ref[f * FRAME : (f + 1) * FRAME, :], g, NT)
            total = total + jnp.sum(e, axis=0, keepdims=True)
            delta = delta + jnp.sum(e * dp, axis=0, keepdims=True)
            e_scr[n] = e
            dp_scr[n] = dp
        inverse = jnp.where(total > 0.0, 1.0 / total, 0.0)
        delta = delta * inverse
        for n, f in enumerate(keys):
            p = e_scr[n] * inverse
            ds = (p * (dp_scr[n] - delta)).astype(jnp.bfloat16)
            rows = slice((f + RADIUS) * FRAME, (f + RADIUS + 1) * FRAME)
            dv_acc[rows, :] += dot(p.astype(jnp.bfloat16), g, NN)
            dk_acc[rows, :] += dot(ds, q, NN)
    dk_ref[...] = (dk_acc[pl.ds(rim, own), :] * scale).astype(jnp.bfloat16)
    dv_ref[...] = dv_acc[pl.ds(rim, own), :].astype(jnp.bfloat16)


VM = pl.BlockSpec(memory_space=pltpu.VMEM)
SM = pl.BlockSpec(memory_space=pltpu.SMEM)


def stats_call(where, radius, clip_ids, q, k, v, g):
    rows, width = q.shape
    count = rows // FRAME
    out = jax.ShapeDtypeStruct((RADIUS * FRAME + STAT_ROWS, width), jnp.bfloat16)
    return pl.pallas_call(
        functools.partial(stats_kernel, count),
        out_shape=(out, out),
        in_specs=[SM] * 3 + [VM] * 4,
        out_specs=(VM, VM),
        scratch_shapes=[
            pltpu.VMEM((2 * RADIUS, FRAME, FRAME), jnp.float32),
            pltpu.VMEM((STAT_ROWS, width), jnp.float32),
        ],
        cost_estimate=pl.CostEstimate(flops=16 * 4 * FRAME * FRAME * width, bytes_accessed=5 * rows * width, transcendentals=0),
        name="rim_stats",
    )(where, radius, clip_ids, q, k, v, g)


def main_call(where, radius, clip_ids, q, k, v, g, odd, even, relay, godd, geven):
    rows, width = q.shape
    count = rows // FRAME
    ext = rows + 2 * RADIUS * FRAME
    out = jax.ShapeDtypeStruct((rows, width), jnp.bfloat16)
    return pl.pallas_call(
        functools.partial(main_kernel, count),
        out_shape=(out, out, out),
        in_specs=[SM] * 3 + [VM] * 9,
        out_specs=(VM, VM, VM),
        scratch_shapes=[
            pltpu.VMEM((ext, width), jnp.bfloat16),
            pltpu.VMEM((ext, width), jnp.bfloat16),
            pltpu.VMEM((2 * RADIUS * FRAME, width), jnp.bfloat16),
            pltpu.VMEM((2 * RADIUS * FRAME, width), jnp.bfloat16),
            pltpu.VMEM((width, ext), jnp.bfloat16),
            pltpu.VMEM((ext, width), jnp.float32),
            pltpu.VMEM((ext, width), jnp.float32),
            pltpu.VMEM((SPAN, FRAME, FRAME), jnp.float32),
            pltpu.VMEM((SPAN, FRAME, FRAME), jnp.float32),
            pltpu.VMEM((2 * STAT_ROWS, width), jnp.float32),
        ],
        cost_estimate=pl.CostEstimate(flops=46 * 10 * FRAME * FRAME * width, bytes_accessed=14 * rows * width, transcendentals=0),
        name="band_grads",
    )(where, radius, clip_ids, q, k, v, g, odd, even, relay, godd, geven)


def both_ways(pairs):
    return pairs + [(b, a) for a, b in pairs]


def exchange_pairs(size, plane):
    odd = both_ways([(i, i + 1) for i in range(1, size - 1, 2)])
    even = both_ways([(i, i + 1) for i in range(0, size - 1, 2)])
    far = [(i, i + 1) for i in range(plane - 1, size - 1, plane)]
    near_odd = [p for p in odd if p not in both_ways(far)]
    first, second, third = [], [], []
    for a, b in far:
        low, high = a - plane + 1, b + plane - 1
        first += [(a, low), (b, high)]
        second += [(low, b), (high, a)]
        third += [(a - 1, b), (b + 1, a)]
    return odd, near_odd, even, far, first, second, third


def per_device(queries, saved_keys, saved_values, out_grad, radius, clip_ids):
    size = lax.axis_size("tm")
    tm = lax.axis_index("tm")
    rows = queries.shape[0]
    rim = RADIUS * FRAME
    parity = tm % 2
    odd_pairs, near_pairs, even_pairs, far_pairs, hop_a1, hop_a2, hop_b2 = exchange_pairs(size, 8)
    is_far = sum((tm == i).astype(jnp.int32) for pair in far_pairs for i in pair)
    where = jnp.stack([tm.astype(jnp.int32), is_far])

    def rim_of(x, slot):
        last = parity if slot == 0 else 1 - parity
        return lax.dynamic_slice_in_dim(x, last * (rows - rim), rim, 0)

    grads = lax.all_to_all(out_grad, "head", split_axis=1, concat_axis=0, tiled=True)
    k_odd, v_odd, q_odd = (rim_of(x, 0) for x in (saved_keys, saved_values, queries))
    relay_v = lax.ppermute(v_odd, "tm", hop_a1)
    even = lax.ppermute(jnp.concatenate([rim_of(x, 1) for x in (saved_keys, saved_values, queries)] + [q_odd], 0), "tm", even_pairs)
    odd_k = lax.ppermute(k_odd, "tm", odd_pairs)
    odd_vq = lax.ppermute(jnp.concatenate([v_odd, q_odd], 0), "tm", near_pairs)
    relay_v = lax.ppermute(relay_v, "tm", hop_a2)
    relay_q = lax.ppermute(even[3 * rim :], "tm", hop_b2)
    relay = jnp.concatenate([relay_v, relay_q], 0)
    odd = jnp.concatenate([odd_k, odd_vq], 0)
    godd, geven = stats_call(where, radius, clip_ids, queries, saved_keys, saved_values, grads)
    godd = lax.ppermute(godd, "tm", odd_pairs)
    geven = lax.ppermute(geven, "tm", even_pairs)
    return main_call(where, radius, clip_ids, queries, saved_keys, saved_values, grads, odd, even, relay, godd, geven)


def solution(mesh):
    placed = (P("tm", "head"),) * 3 + (P(("tm", "head"), None), P("head"), P())
    return jax.shard_map(
        per_device,
        mesh=mesh,
        in_specs=placed,
        out_specs=(P("tm", "head"),) * 3,
        check_vma=False,
    )
```

```python
import functools

import jax
import jax.numpy as jnp
from jax import lax
from jax.experimental import pallas as pl
from jax.experimental.pallas import tpu as pltpu
from jax.sharding import PartitionSpec as P


FRAME = 256
RADIUS = 2
SPAN = 2 * RADIUS + 1
NEG = -1e30
LOG2E = 1.4426950408889634
STAT_ROWS = 48
STATS_VMEM, OWN_VMEM, RIM_VMEM = 16, 32, 16

NT = (((1,), (1,)), ((), ()))
NN = (((1,), (0,)), ((), ()))


def dot(a, b, dims):
    return lax.dot_general(a, b, dims, preferred_element_type=jnp.float32)


def make_allowed(where_ref, radius_ref, clip_ref, count):
    first = where_ref[0] * count
    total = clip_ref.shape[0]
    radius = radius_ref[0]

    def allowed(query, key):
        fq = first + query
        fk = first + key
        inside = (fq >= 0) & (fq < total) & (fk >= 0) & (fk < total)
        cq = clip_ref[jnp.clip(fq, 0, total - 1)]
        ck = clip_ref[jnp.clip(fk, 0, total - 1)]
        return inside & (abs(query - key) <= radius) & (cq == ck)

    return allowed


def block(ref, index):
    return ref[index * FRAME : (index + 1) * FRAME, :]


def raw_scores(keys, q, s_scr, valid, top):
    for n, key in enumerate(keys):
        s = dot(key, q, NT)
        s_scr[n] = s
        peak = jnp.where(valid[n], jnp.max(s, axis=0, keepdims=True), NEG)
        top = peak if top is None else jnp.maximum(top, peak)
    return top


def exponentials(values, g, s_scr, dp_scr, valid, top, total, delta, c, keep):
    for n, value in enumerate(values):
        shift = jnp.where(valid[n], top, -NEG)
        e = jnp.exp2((s_scr[n] - shift) * c)
        dp = dot(value, g, NT)
        total = total + jnp.sum(e, axis=0, keepdims=True)
        delta = delta + jnp.sum(e * dp, axis=0, keepdims=True)
        if keep:
            s_scr[n] = e
            dp_scr[n] = dp
    return total, delta


def stats_kernel(count, where_ref, radius_ref, clip_ref, q_ref, k_ref, v_ref, g_ref, odd_ref, even_ref, s_scr, row_scr, out_scr):
    c = q_ref.shape[1] ** -0.5 * LOG2E
    allowed = make_allowed(where_ref, radius_ref, clip_ref, count)
    parity = lax.rem(where_ref[0], 2)
    row_scr[...] = jnp.zeros_like(row_scr)
    jobs = []
    for side in range(2):
        for i in range(RADIUS):
            qf = side * (count - RADIUS) + i
            keys = [f for f in range(qf - RADIUS, qf + RADIUS + 1) if 0 <= f < count]
            jobs.append((side, i, qf, keys))
    tops = {}

    def begin(n):
        _, _, qf, keys = jobs[n]
        valid = [allowed(qf, f) for f in keys]
        top = raw_scores([block(k_ref, f) for f in keys], block(q_ref, qf), s_scr.at[n], valid, None)
        tops[n] = (valid, top)

    def finish(n):
        side, i, qf, keys = jobs[n]
        valid, top = tops[n]
        zero = jnp.zeros_like(top)
        g = block(g_ref, qf)
        out_scr[side, i * FRAME : (i + 1) * FRAME, :] = g
        total, delta = exponentials([block(v_ref, f) for f in keys], g, s_scr.at[n], None, valid, top, zero, zero, c, False)
        row = side * STAT_ROWS + i * 18
        for stat in (top, total, delta):
            rest = stat
            for _ in range(3):
                part = rest.astype(jnp.bfloat16).astype(jnp.float32)
                rest = rest - part
                row_scr[row : row + 1, :] = part[:, :128]
                row_scr[row + 1 : row + 2, :] = part[:, 128:]
                row += 2

    begin(0)
    for n in range(len(jobs)):
        if n + 1 < len(jobs):
            begin(n + 1)
        finish(n)
    for side in range(2):
        out_scr[side, RADIUS * FRAME :, :] = row_scr[side * STAT_ROWS : (side + 1) * STAT_ROWS, :].astype(jnp.bfloat16)
    odd_ref[...] = out_scr[parity]
    even_ref[...] = out_scr[1 - parity]


def own_kernel(
    count,
    where_ref,
    radius_ref,
    clip_ref,
    q_ref,
    k_ref,
    v_ref,
    g_ref,
    kodd_ref,
    vodd_ref,
    vrelay_ref,
    keven_ref,
    veven_ref,
    dq_ref,
    dk_ref,
    dv_ref,
    dk_part,
    dv_part,
    kx,
    vx,
    kt,
    dk_acc,
    dv_acc,
    s_scr,
    dp_scr,
):
    scale = q_ref.shape[1] ** -0.5
    c = scale * LOG2E
    allowed = make_allowed(where_ref, radius_ref, clip_ref, count)
    parity = lax.rem(where_ref[0], 2)
    kx[parity] = kodd_ref[...]
    vx[parity] = vodd_ref[...]
    kx[1 - parity] = keven_ref[...]
    vx[1 - parity] = veven_ref[...]

    @pl.when(where_ref[1] == 1)
    def _():
        vx[parity] = vrelay_ref[...]

    def frame_of(own_ref, halo, f):
        if 0 <= f < count:
            return block(own_ref, f)
        side, i = (0, f + RADIUS) if f < 0 else (1, f - count)
        return halo[side, i * FRAME : (i + 1) * FRAME, :]

    def turn(f):
        kt[:, (f + RADIUS) * FRAME : (f + RADIUS + 1) * FRAME] = frame_of(k_ref, kx, f).T

    tops = {}

    def begin(a):
        keys = range(a - RADIUS, a + RADIUS + 1)
        valid = [True if f == a else allowed(a, f) for f in keys]
        top = raw_scores([frame_of(k_ref, kx, f) for f in keys], block(q_ref, a), s_scr.at[a % 2], valid, None)
        tops[a] = (valid, top)

    begin(0)
    for f in range(-RADIUS, RADIUS):
        turn(f)
    for a in range(count):
        if a + 1 < count:
            begin(a + 1)
        turn(a + RADIUS)
        keys = list(range(a - RADIUS, a + RADIUS + 1))
        valid, top = tops[a]
        q = block(q_ref, a)
        g = block(g_ref, a)
        zero = jnp.zeros_like(top)
        s_a, dp_a = s_scr.at[a % 2], dp_scr.at[a % 2]
        total, delta = exponentials([frame_of(v_ref, vx, f) for f in keys], g, s_a, dp_a, valid, top, zero, zero, c, True)
        inverse = 1.0 / total
        delta = delta * inverse
        dqt = None
        for n, f in enumerate(keys):
            p = s_a[n] * inverse
            ds = (p * (dp_a[n] - delta)).astype(jnp.bfloat16)
            part = dot(kt[:, (f + RADIUS) * FRAME : (f + RADIUS + 1) * FRAME], ds, NN)
            dqt = part if dqt is None else dqt + part
            if not 0 <= f < count:
                continue
            dv = dot(p.astype(jnp.bfloat16), g, NN)
            dk = dot(ds, q, NN)
            rows = slice(f * FRAME, (f + 1) * FRAME)
            if a > max(0, f - RADIUS):
                dv = dv + dv_acc[rows, :]
                dk = dk + dk_acc[rows, :]
            if a < min(count - 1, f + RADIUS):
                dv_acc[rows, :] = dv
                dk_acc[rows, :] = dk
            elif RADIUS <= f < count - RADIUS:
                dv_ref[rows, :] = dv.astype(jnp.bfloat16)
                dk_ref[rows, :] = (dk * scale).astype(jnp.bfloat16)
            else:
                at = f if f < RADIUS else f - count + 2 * RADIUS
                part_rows = slice(at * FRAME, (at + 1) * FRAME)
                dv_part[part_rows, :] = dv
                dk_part[part_rows, :] = dk
                dv_ref[rows, :] = dv.astype(jnp.bfloat16)
                dk_ref[rows, :] = dk.astype(jnp.bfloat16)
        dq_ref[a * FRAME : (a + 1) * FRAME, :] = (dqt * scale).T.astype(jnp.bfloat16)


def rim_kernel(
    count,
    where_ref,
    radius_ref,
    clip_ref,
    k_ref,
    v_ref,
    dk_part,
    dv_part,
    qodd_ref,
    qrelay_ref,
    qeven_ref,
    godd_ref,
    geven_ref,
    dk_in,
    dv_in,
    dk_ref,
    dv_ref,
    qx,
    gx,
    s_scr,
    dp_scr,
):
    scale = k_ref.shape[1] ** -0.5
    c = scale * LOG2E
    rim = RADIUS * FRAME
    allowed = make_allowed(where_ref, radius_ref, clip_ref, count)
    parity = lax.rem(where_ref[0], 2)
    side_now = pl.program_id(0)

    @pl.when(parity == side_now)
    def _():
        qx[...] = qodd_ref[...]
        gx[...] = godd_ref[...]

    @pl.when((parity == side_now) & (where_ref[1] == 1))
    def _():
        qx[...] = qrelay_ref[...]

    @pl.when(parity != side_now)
    def _():
        qx[...] = qeven_ref[...]
        gx[...] = geven_ref[...]

    def one_side(side):
        stat = gx[rim:, :].astype(jnp.float32)
        sums = [None] * RADIUS
        state = {}
        for i in range(RADIUS):
            qf = i - RADIUS if side == 0 else count + i
            slots = list(range(0, i + 1)) if side == 0 else list(range(i, RADIUS))
            frames = slots if side == 0 else [f + count - RADIUS for f in slots]
            stats = []
            row = i * 18
            for _ in range(3):
                halves = [stat[row + n : row + n + 1] + stat[row + 2 + n : row + 3 + n] + stat[row + 4 + n : row + 5 + n] for n in range(2)]
                stats.append(jnp.concatenate(halves, axis=1))
                row += 6
            valid = [allowed(qf, f) for f in frames]
            top = raw_scores([block(k_ref, n) for n in slots], block(qx, i), s_scr.at[i], valid, stats[0])
            state[i] = (slots, valid, stats, top)
        for i in range(RADIUS):
            slots, valid, (far_top, total, delta), top = state[i]
            q, g = block(qx, i), block(gx, i)
            s_i, dp_i = s_scr.at[i], dp_scr.at[i]
            fade = jnp.exp2((far_top - top) * c)
            total, delta = exponentials([block(v_ref, n) for n in slots], g, s_i, dp_i, valid, top, total * fade, delta * fade, c, True)
            inverse = jnp.where(total > 0.0, 1.0 / total, 0.0)
            delta = delta * inverse
            for n, slot in enumerate(slots):
                p = s_i[n] * inverse
                ds = (p * (dp_i[n] - delta)).astype(jnp.bfloat16)
                dv = dot(p.astype(jnp.bfloat16), g, NN)
                dk = dot(ds, q, NN)
                old = sums[slot]
                sums[slot] = (dv, dk) if old is None else (old[0] + dv, old[1] + dk)
        for slot in range(RADIUS):
            rows = slice(slot * FRAME, (slot + 1) * FRAME)
            dv_ref[rows, :] = (dv_part[rows, :] + sums[slot][0]).astype(jnp.bfloat16)
            dk_ref[rows, :] = ((dk_part[rows, :] + sums[slot][1]) * scale).astype(jnp.bfloat16)

    for side in range(2):
        pl.when(side_now == side)(functools.partial(one_side, side))


VM = pl.BlockSpec(memory_space=pltpu.VMEM)
SM = pl.BlockSpec(memory_space=pltpu.SMEM)
MIB = 1 << 20


def piece(rows, width, index):
    return pl.BlockSpec((rows, width), lambda i: (index, 0))


def stats_call(scalars, q, k, v, g):
    rows, width = q.shape
    count = rows // FRAME
    out = jax.ShapeDtypeStruct((RADIUS * FRAME + STAT_ROWS, width), jnp.bfloat16)
    return pl.pallas_call(
        functools.partial(stats_kernel, count),
        out_shape=(out, out),
        in_specs=[SM] * 3 + [VM] * 4,
        out_specs=(VM, VM),
        scratch_shapes=[
            pltpu.VMEM((2 * RADIUS, 2 * RADIUS, FRAME, FRAME), jnp.float32),
            pltpu.VMEM((2 * STAT_ROWS, width), jnp.float32),
            pltpu.VMEM((2, RADIUS * FRAME + STAT_ROWS, width), jnp.bfloat16),
        ],
        compiler_params=pltpu.CompilerParams(vmem_limit_bytes=STATS_VMEM * MIB),
        cost_estimate=pl.CostEstimate(flops=14 * 4 * FRAME * FRAME * width, bytes_accessed=5 * rows * width, transcendentals=0),
        name="rim_stats",
    )(*scalars, q, k, v, g)


def own_call(scalars, q, k, v, g, kodd, vqodd, vrelay, even):
    rows, width = q.shape
    count = rows // FRAME
    rim = RADIUS * FRAME
    out = jax.ShapeDtypeStruct((rows, width), jnp.bfloat16)
    part = jax.ShapeDtypeStruct((2 * rim, width), jnp.float32)
    whole = piece(rows, width, 0)
    half = piece(rim, width, 0)
    return pl.pallas_call(
        functools.partial(own_kernel, count),
        out_shape=(out, out, out, part, part),
        grid=(1,),
        in_specs=[SM] * 3 + [whole] * 4 + [half, half, half, half, piece(rim, width, 1)],
        out_specs=(whole, whole, whole, piece(2 * rim, width, 0), piece(2 * rim, width, 0)),
        scratch_shapes=[
            pltpu.VMEM((2, rim, width), jnp.bfloat16),
            pltpu.VMEM((2, rim, width), jnp.bfloat16),
            pltpu.VMEM((width, rows + 2 * rim), jnp.bfloat16),
            pltpu.VMEM((rows, width), jnp.float32),
            pltpu.VMEM((rows, width), jnp.float32),
            pltpu.VMEM((2, SPAN, FRAME, FRAME), jnp.float32),
            pltpu.VMEM((2, SPAN, FRAME, FRAME), jnp.float32),
        ],
        compiler_params=pltpu.CompilerParams(vmem_limit_bytes=OWN_VMEM * MIB),
        cost_estimate=pl.CostEstimate(flops=40 * 10 * FRAME * FRAME * width, bytes_accessed=14 * rows * width, transcendentals=0),
        name="own_rows",
    )(*scalars, q, k, v, g, kodd, vqodd, vrelay, even, even)


def rim_call(scalars, k, v, dk_part, dv_part, vqodd, qrelay, even, godd, geven, dk, dv):
    rows, width = k.shape
    count = rows // FRAME
    rim = RADIUS * FRAME
    out = jax.ShapeDtypeStruct((rows, width), jnp.bfloat16)
    edge = pl.BlockSpec((rim, width), lambda i: (i * (count // RADIUS - 1), 0))
    part = pl.BlockSpec((rim, width), lambda i: (i, 0))
    grads = piece(rim + STAT_ROWS, width, 0)
    untouched = pl.BlockSpec(memory_space=pl.ANY)
    return pl.pallas_call(
        functools.partial(rim_kernel, count),
        out_shape=(out, out),
        grid=(2,),
        in_specs=[SM] * 3
        + [edge, edge, part, part, piece(rim, width, 1), piece(rim, width, 0), piece(rim, width, 2), grads, grads]
        + [untouched] * 2,
        out_specs=(edge, edge),
        input_output_aliases={12: 0, 13: 1},
        scratch_shapes=[
            pltpu.VMEM((rim, width), jnp.bfloat16),
            pltpu.VMEM((rim + STAT_ROWS, width), jnp.bfloat16),
            pltpu.VMEM((RADIUS, RADIUS, FRAME, FRAME), jnp.float32),
            pltpu.VMEM((RADIUS, RADIUS, FRAME, FRAME), jnp.float32),
        ],
        compiler_params=pltpu.CompilerParams(vmem_limit_bytes=RIM_VMEM * MIB),
        cost_estimate=pl.CostEstimate(flops=6 * 8 * FRAME * FRAME * width, bytes_accessed=6 * rows * width, transcendentals=0),
        name="rim_rows",
    )(*scalars, k, v, dk_part, dv_part, vqodd, qrelay, even, godd, geven, dk, dv)


def both_ways(pairs):
    return pairs + [(b, a) for a, b in pairs]


def exchange_pairs(size, plane):
    odd = both_ways([(i, i + 1) for i in range(1, size - 1, 2)])
    even = both_ways([(i, i + 1) for i in range(0, size - 1, 2)])
    far = [(i, i + 1) for i in range(plane - 1, size - 1, plane)]
    near_odd = [p for p in odd if p not in both_ways(far)]
    first, second, third = [], [], []
    for a, b in far:
        low, high = a - plane + 1, b + plane - 1
        first += [(a, low), (b, high)]
        second += [(low, b), (high, a)]
        third += [(a - 1, b), (b + 1, a)]
    return odd, near_odd, even, far, first, second, third


def per_device(queries, saved_keys, saved_values, out_grad, radius, clip_ids):
    size = lax.axis_size("tm")
    tm = lax.axis_index("tm")
    rows = queries.shape[0]
    rim = RADIUS * FRAME
    parity = tm % 2
    odd_pairs, near_pairs, even_pairs, far_pairs, hop_a1, hop_a2, hop_b2 = exchange_pairs(size, 8)
    is_far = sum((tm == i).astype(jnp.int32) for pair in far_pairs for i in pair)
    where = jnp.stack([tm.astype(jnp.int32), is_far])

    def rim_of(x, slot):
        last = parity if slot == 0 else 1 - parity
        return lax.dynamic_slice_in_dim(x, last * (rows - rim), rim, 0)

    grads = lax.all_to_all(out_grad, "head", split_axis=1, concat_axis=0, tiled=True)
    k_odd, v_odd, q_odd = (rim_of(x, 0) for x in (saved_keys, saved_values, queries))
    relay_v = lax.ppermute(v_odd, "tm", hop_a1)
    even = lax.ppermute(jnp.concatenate([rim_of(x, 1) for x in (saved_keys, saved_values, queries)] + [q_odd], 0), "tm", even_pairs)
    odd_k = lax.ppermute(k_odd, "tm", odd_pairs)
    odd_vq = lax.ppermute(jnp.concatenate([v_odd, q_odd], 0), "tm", near_pairs)
    relay_v = lax.ppermute(relay_v, "tm", hop_a2)
    relay_q = lax.ppermute(even[3 * rim :], "tm", hop_b2)
    scalars = (where, radius, clip_ids)
    godd, geven = stats_call(scalars, queries, saved_keys, saved_values, grads)
    godd = lax.ppermute(godd, "tm", odd_pairs)
    geven = lax.ppermute(geven, "tm", even_pairs)
    dq, dk, dv, dk_part, dv_part = own_call(scalars, queries, saved_keys, saved_values, grads, odd_k, odd_vq, relay_v, even)
    dk, dv = rim_call(scalars, saved_keys, saved_values, dk_part, dv_part, odd_vq, relay_q, even, godd, geven, dk, dv)
    return dq, dk, dv


def solution(mesh):
    placed = (P("tm", "head"),) * 3 + (P(("tm", "head"), None), P("head"), P())
    return jax.shard_map(
        per_device,
        mesh=mesh,
        in_specs=placed,
        out_specs=(P("tm", "head"),) * 3,
        check_vma=False,
    )
```
